128 devices in a mesh: grp: 32 (over y_lo, z, x), blk: 4 (over y_hi, core).
Axes of the slice: x: 4, y: 4 (y_hi: 2, y_lo: 2; y = y_hi * 2 + y_lo), z: 4, core: 2. Of those that a mesh axis runs over, the one named last changes fastest.
Arguments:
- embeddings: bfloat16 [196608, 768], P(('grp', 'blk')), may hold values from -6 to 6
- route: int32 [196608], P(('grp', 'blk')), may hold values from 0 to 196607, as said below
- cluster: int32 [32, 6144], P('grp', 'blk'), may hold values from 0 to 3, never falling along the last dimension, each value on 1 to 3072 neighbouring positions
Outputs:
- best_cosine: float32 [196608], P(('grp', 'blk'))
The draws below stay inside these ranges and needn't reach their ends.
Inputs may be any that keep to these rules, and one draw needn't show every extreme that they name: route is a permutation of all slots; the 1536 rows of each device are sent to every device's 1536 slots in exactly 12 cases, and which rows and which slots is drawn from the seed. Within each family the cluster numbers never fall along the slots, every cluster number occurs, and one cluster has exactly 3072 slots.
All inputs are finite; a program needn't handle non-finite values.
Results may differ from the reference program's by a relative error of at most 0.0014.
Values may be sent and summed in bfloat16 or wider, within the bound.
A program may use at most 64 MiB of HBM per device.

```python
import math
import jax
import jax.numpy as jnp
import numpy as np
from jax import lax

D = 768
ROW_DEV = 1536
CLUSTERS_GRP = 4
GROUP_ROWS = 6144
MOST = 3072
ROWS = 196608
N_GRP = 32


def draw_route(key, part):
    device_count = ROWS // ROW_DEV
    pair_rows = ROW_DEV // device_count
    source_keys = jax.random.split(jax.random.fold_in(key, 11), device_count)
    target_keys = jax.random.split(jax.random.fold_in(key, 12), device_count)
    source_perm = jax.vmap(lambda piece: jax.random.permutation(piece, ROW_DEV))(source_keys).astype(jnp.int32)
    target_perm = jax.vmap(lambda piece: jax.random.permutation(piece, ROW_DEV))(target_keys).astype(jnp.int32)
    destination = source_perm // pair_rows
    within_pair = source_perm % pair_rows
    sources = jnp.arange(device_count, dtype=jnp.int32)[:, None]
    slot_pos = target_perm[destination, sources * pair_rows + within_pair]
    return (destination * ROW_DEV + slot_pos).reshape(-1).astype(jnp.int32)


def block_scale(rng, extent, cuts, low, largest):
    loudness, own = 1.0, jax.random.fold_in(rng, 6)
    for dim, blocks in cuts:
        draws = jnp.exp(jax.random.uniform(jax.random.fold_in(own, dim), (blocks,), jnp.float32, low / len(cuts), largest / len(cuts)))
        loudness = loudness * jnp.repeat(draws, extent[dim] // blocks).reshape([-1 if axis == dim else 1 for axis in range(len(extent))])
    return loudness


def profile(number_of, total, limit, slope):
    weights = [(1 << 20) // math.isqrt(standing ** slope) + 1 for standing in range(2, number_of + 1)]
    surplus, given = total - limit - (number_of - 1), [1] * (number_of - 1)
    while surplus > 0:
        candidates = [i for i in range(number_of - 1) if given[i] < limit]
        pool, left = sum([weights[i] for i in candidates]), surplus
        for i in candidates:
            addition = min(limit - given[i], max(1, left * weights[i] // pool), surplus)
            given[i] = given[i] + addition
            surplus = surplus - addition
    return np.array([limit] + given)


def uneven_parts(key, count, total, reach, skew):
    if count == 2:
        one = jax.random.randint(key, (), max(1, total - reach), min(reach, total - 1) + 1)
        return jnp.stack([one, total - one])
    lengths = jnp.asarray(profile(count, total, reach, skew), jnp.int32)
    twos = (count - 1) // 2
    donor, receiver = lengths[1:1 + 2 * twos:2], lengths[2:2 + 2 * twos:2]
    margin = jnp.minimum(donor - 1, reach - receiver)
    moved = jax.random.randint(jax.random.fold_in(key, 1), (twos,), 0, 1 << 20) % (margin + 1)
    lengths = lengths.at[1:1 + 2 * twos:2].set(donor - moved).at[2:2 + 2 * twos:2].set(receiver + moved)
    return lengths[jax.random.permutation(jax.random.fold_in(key, 2), count)]


def bell_draw(own_key, shape, width, most, cuts=(), kind=jnp.bfloat16):
    array = width * jax.random.normal(own_key, shape, jnp.float32)
    if cuts:
        array = array * block_scale(own_key, shape, cuts, -0.22, 0.18)
    return jnp.clip(array, -most, most).astype(kind)


def setup_inputs(seed: int = 0) -> dict:
    arg_keys = jax.random.split(jax.random.key(seed), 4)
    return {
        "embeddings": bell_draw(arg_keys[0], (ROWS, D), 1.0, 6.0, ((0, 128),)),
        "route": draw_route(jax.random.fold_in(arg_keys[3], 71), 0),
        "cluster": jax.vmap(lambda own: jnp.searchsorted(jnp.cumsum(uneven_parts(own, CLUSTERS_GRP, GROUP_ROWS, MOST, 2)), jnp.arange(GROUP_ROWS), side="right"))(jax.random.split(arg_keys[2], N_GRP)).reshape((N_GRP, GROUP_ROWS)).astype(jnp.int32),
    }


def family_scores(group_unit, group_index, group_cluster):
    total_rows = group_unit.shape[0]
    block_rows = 512 if total_rows % 512 == 0 else total_rows

    def one_block(start):
        unit_part = lax.dynamic_slice_in_dim(group_unit, start, block_rows, 0)
        index_part = lax.dynamic_slice_in_dim(group_index, start, block_rows, 0)
        cluster_part = lax.dynamic_slice_in_dim(group_cluster, start, block_rows, 0)
        scores = jnp.dot(unit_part, group_unit.T, preferred_element_type=jnp.float32)
        matches = (cluster_part[:, None] == group_cluster[None, :]) & (group_index[None, :] < index_part[:, None])
        floor_value = jnp.full(scores.shape, -1.0, scores.dtype)
        return lax.optimization_barrier(jnp.max(jnp.where(matches, scores, floor_value), axis=1))
    starts = jnp.arange(total_rows // block_rows, dtype=jnp.int32) * block_rows
    return lax.map(one_block, starts).reshape(total_rows)

def reference(embeddings, route, cluster):
    values = embeddings.astype(jnp.float32)
    unit_rows = (values * lax.rsqrt(lax.optimization_barrier(jnp.sum(values * values, axis=1, keepdims=True)) + 1e-06)).astype(jnp.bfloat16)
    positions = jnp.arange(ROWS, dtype=jnp.int32)
    slot_unit = jnp.zeros_like(unit_rows).at[route].set(unit_rows)
    slot_index = jnp.zeros((ROWS,), jnp.int32).at[route].set(positions)
    slot_best = lax.map(lambda packed: family_scores(packed[0], packed[1], packed[2]), (slot_unit.reshape(N_GRP, GROUP_ROWS, D), slot_index.reshape(N_GRP, GROUP_ROWS), cluster))
    return slot_best.reshape(ROWS)[route]
```

```python
import functools

import jax
import jax.numpy as jnp
from jax import lax
from jax.experimental import pallas as pl
from jax.experimental.pallas import tpu as pltpu
from jax.sharding import PartitionSpec as P

MESH = pl.DeviceIdType.MESH
F32, BF16, I32 = jnp.float32, jnp.bfloat16, jnp.int32
SLAB = 40
USED = 36
WINDOWS = 8
CHUNK = 16 * SLAB


def dot(a, b):
    return lax.dot_general(a, b, (((1,), (0,)), ((), ())), preferred_element_type=F32)


def dot_t(a, b):
    return lax.dot_general(a, b, (((1,), (1,)), ((), ())), preferred_element_type=F32)


def iota(shape, dim):
    return lax.broadcasted_iota(I32, shape, dim)


def quotient(value, by):
    return jnp.floor((value + 0.5) * (1.0 / by))


def thirds(value):
    first = value.astype(BF16)
    rest = value - first.astype(F32)
    second = rest.astype(BF16)
    return first, second, (rest - second.astype(F32)).astype(BF16)


def window_shift(w):
    return w // 2, w % 2


def chip_of(u, v, e, x):
    return x, (u + x) % 4, (v + 2 * e + x) % 4


def device_of(x, y, z, core):
    return (y % 2) * 16 + z * 4 + x, (y // 2) * 2 + core


def kernel(
    emb_ref, route_ref, cluster_ref, out_ref,
    unit, send, rows, table, picks, ranks, meta, count, counts, spread, key_col, key_row, cl_col, cl_row, best, gone, back,
    send_sem, recv_sem, pass_sem, pass_send_sem, count_sem, count_send_sem, back_sem, back_send_sem,
):
    row_count, width = emb_ref.shape
    grp, blk = lax.axis_index("grp"), lax.axis_index("blk")
    me = grp * 4 + blk
    y_lo, z0, x0 = grp // 16, (grp // 4) % 4, grp % 4
    y0, core = (blk // 2) * 2 + y_lo, blk % 2
    u0, v0, e0 = (y0 - x0 + 4) % 4, (z0 - x0 + 4) % 2, ((z0 - x0 + 4) % 4) // 2
    sibling = (grp, blk + 1 - 2 * core)

    barrier = pltpu.get_barrier_semaphore()

    def greet(i, carry):
        other = (me + 1 + i) % 128
        pl.semaphore_signal(barrier, inc=1, device_id=(other // 4, other % 4), device_id_type=MESH)
        return carry

    lax.fori_loop(0, 127, greet, 0)

    values = emb_ref[...].astype(F32)
    unit[...] = (values * lax.rsqrt(jnp.sum(values * values, axis=1, keepdims=True) + 1e-06)).astype(BF16)

    route = route_ref[...].astype(F32)
    family = quotient(route, 6144)
    slot = route - family * 6144
    block = quotient(slot, 1536)
    slot_hi = quotient(slot, 48)
    slot_lo = slot - slot_hi * 48
    family_int = family.astype(I32)
    fam_y, fam_z, fam_x = family_int >> 4, (family_int >> 2) & 3, family_int & 3

    def order_number(y):
        dx, dy, dz = (fam_x - x0) & 3, (y - y0) & 3, (fam_z - z0) & 3
        du, dzx = (dy - dx) & 3, (dz - dx) & 3
        return (du * 2 + (dzx & 1)) * 8 + (dzx >> 1) * 4 + dx

    pick_a = jnp.where(block < 2.5, order_number(fam_y), -1)
    pick_b = jnp.where(block > 0.5, order_number(fam_y + 2), -1)
    slab_iota = iota((64, row_count), 0)
    hot_a = (slab_iota == pick_a).astype(F32)
    hot_b = (slab_iota == pick_b).astype(F32)
    hot = (hot_a + hot_b).astype(BF16)
    earlier = (iota((256, 256), 0) < iota((256, 256), 1)).astype(F32).astype(BF16)
    before = jnp.zeros((64, 1), F32)
    prefix = []
    for k in range(row_count // 256):
        part = hot[:, k * 256:(k + 1) * 256]
        prefix.append(dot(part, earlier) + before)
        before = before + jnp.sum(part.astype(F32), axis=1, keepdims=True)
    prefix = jnp.concatenate(prefix, axis=1)
    rank_a = jnp.sum(hot_a * prefix, axis=0, keepdims=True).astype(I32)
    rank_b = jnp.sum(hot_b * prefix, axis=0, keepdims=True).astype(I32)
    picks[0:1, :], picks[1:2, :] = pick_a, pick_b
    ranks[0:1, :], ranks[1:2, :] = rank_a, rank_b
    lane_iota = iota((128, row_count), 0)
    hi = jnp.zeros((64, 128), F32)
    lo = jnp.zeros((64, 128), F32)
    for hot_one, rank in ((hot_a, rank_a), (hot_b, rank_b)):
        chosen = lane_iota == rank
        hi = hi + dot_t(hot_one.astype(BF16), jnp.where(chosen, slot_hi, 0.0).astype(BF16))
        lo = lo + dot_t(hot_one.astype(BF16), jnp.where(chosen, slot_lo, 0.0).astype(BF16))
    meta[0:64, :] = hi.astype(BF16)
    meta[64:128, :] = lo.astype(BF16)

    cluster = cluster_ref[...]
    which = iota((8, 128), 0)
    tally = jnp.zeros((8, 128), F32)
    for k in range(1, 4):
        below = jnp.sum((cluster < k).astype(F32), axis=1, keepdims=True)
        tally = jnp.where(which == k, below, tally)
    count[...] = tally

    pl.semaphore_wait(barrier, 127)

    def count_copy(step):
        return pltpu.make_async_remote_copy(
            src_ref=count, dst_ref=counts.at[step], send_sem=count_send_sem.at[step], recv_sem=count_sem.at[step],
            device_id=(grp, (blk + 1 + step) % 4), device_id_type=MESH,
        )

    for step in range(3):
        count_copy(step).start()

    target_a = jnp.where(pick_a >= 0, pick_a * SLAB + rank_a, -1)
    target_b = jnp.where(pick_b >= 0, pick_b * SLAB + rank_b, -1)
    picks[2:3, :], picks[3:4, :] = target_a, target_b
    home_row = ((v0 * 4 + u0) * 16 + (e0 * 4 + x0) * 2 + core) * (SLAB // 8)
    p_col = iota((8 * SLAB, 128), 0).astype(F32)
    p_slab = quotient(p_col, SLAB)
    p_in = (p_col - p_slab * SLAB).astype(I32)
    p_slab = p_slab.astype(I32)
    p_lane = iota((8 * SLAB, 128), 1)

    def make_window(w, carry):
        p_iota = iota((8 * SLAB, row_count), 0) + w * (8 * SLAB)
        one_hot = ((p_iota == picks[2:3, :]) | (p_iota == picks[3:4, :])).astype(F32).astype(BF16)
        body = dot(one_hot, unit[...])
        slab_no = p_slab + w * 8
        info_hot = (((p_in == USED) & (p_lane == slab_no)) | ((p_in == USED + 1) & (p_lane == slab_no + 64))).astype(F32).astype(BF16)
        info = dot(info_hot, meta[...])
        base = w * SLAB
        body = jnp.concatenate([body[:, 0:128] + info, body[:, 128:width]], axis=1).astype(BF16)
        send[pl.ds(base, SLAB)] = body.reshape(SLAB, 8, width)
        du, dv = window_shift(w)

        def send_one(k, inner):
            dx, dy, dz = chip_of(du, dv, k // 4, k % 4)
            to = device_of((x0 + dx) % 4, (y0 + dy) % 4, (z0 + dz) % 4, v0)
            source = send.at[pl.ds((w * 8 + k) * (SLAB // 8), SLAB // 8)]
            here = (to[0] * 4 + to[1]) == me

            @pl.when(jnp.logical_not(here))
            def _():
                pltpu.make_async_remote_copy(
                    src_ref=source, dst_ref=rows.at[pl.ds(home_row, SLAB // 8)], send_sem=send_sem, recv_sem=recv_sem.at[w],
                    device_id=to, device_id_type=MESH,
                ).start()

            @pl.when(here)
            def _():
                pltpu.make_async_copy(source, rows.at[pl.ds(home_row, SLAB // 8)], recv_sem.at[w]).start()

            return inner

        lax.fori_loop(0, 8, send_one, 0)
        return carry

    lax.fori_loop(0, WINDOWS, make_window, 0)

    p = iota((CHUNK, 128), 0).astype(F32)
    slab_of = quotient(p, SLAB)
    in_slab = p - slab_of * SLAB
    diagonal = ((iota((CHUNK, 128), 1).astype(F32) == in_slab) & (in_slab < USED)).astype(F32)
    other = iota((CHUNK, CHUNK), 1).astype(F32)
    p_wide = iota((CHUNK, CHUNK), 0).astype(F32)
    first = quotient(p_wide, SLAB) * SLAB
    spread[...] = jnp.where(other == first + USED, 48.0, jnp.where(other == first + (USED + 1), 1.0, 0.0)).astype(BF16)

    def data_key(slab_no, inside, u, v):
        sx, se, sc = (slab_no >> 1) & 3, slab_no >> 3, slab_no & 1
        sy, sz = (u + sx) & 3, (v + 2 * se + sx) & 3
        source = ((sy & 1) * 16 + sz * 4 + sx) * 4 + (sy >> 1) * 2 + sc
        return source * SLAB + inside

    slab_col, in_col = slab_of.astype(I32), in_slab.astype(I32)
    q = iota((8, CHUNK), 1).astype(F32)
    slab_row = quotient(q, SLAB)
    in_row = (q - slab_row * SLAB).astype(I32)
    slab_row = slab_row.astype(I32)

    def make_keys(k, carry):
        key_col[k] = data_key(slab_col, in_col, k % 4, k // 4)
        key_row[k] = data_key(slab_row, in_row, k % 4, k // 4)
        return carry

    lax.fori_loop(0, WINDOWS, make_keys, 0)
    best[...] = jnp.full(best.shape, -1.0, F32)

    total = count[...]
    for step in range(3):
        count_copy(step).wait()
        total = total + counts[step]
    ends = [total[k:k + 1, :] for k in range(1, 4)]
    ones_col = jnp.ones((128, 128), BF16)
    ones_row = jnp.ones((8, 128), BF16)

    def chunk_of(w):
        du, dv = window_shift(w)
        u, v = (u0 - du + 4) % 4, (v0 - dv + 2) % 2
        return v * 4 + u, v

    def pass_copy(w, chunk):
        part = rows.at[pl.ds(chunk * (CHUNK // 8), CHUNK // 8)]
        return pltpu.make_async_remote_copy(
            src_ref=part, dst_ref=part, send_sem=pass_send_sem.at[w], recv_sem=pass_sem.at[w],
            device_id=sibling, device_id_type=MESH,
        )

    def fold(mine, others):
        x_mine = table[mine]
        x_other = table[others]
        scores = dot_t(x_other, x_mine)
        wide = lambda a: jnp.concatenate([a] * (CHUNK // 128), axis=1)
        same = wide(cl_col[others]) == cl_row[mine][0:1, :]
        prior = wide(key_col[others]) < key_row[mine][0:1, :]
        held = jnp.where(same & prior, scores, -1.0).reshape(CHUNK // 8, 8, CHUNK)
        u = mine % 4
        best[u] = jnp.maximum(best[u], jnp.max(held, axis=0))

    def take_window(w, carry):
        chunk, v = chunk_of(w)
        part = rows.at[pl.ds(chunk * (CHUNK // 8), CHUNK // 8)]

        @pl.when(v == core)
        def _():
            pltpu.make_async_copy(part, part, recv_sem.at[w]).wait()
            pass_copy(w, chunk).start()

        @pl.when(v != core)
        def _():
            pltpu.make_async_copy(part, part, pass_sem.at[w]).wait()

        table[chunk] = rows[pl.ds(chunk * (CHUNK // 8), CHUNK // 8)].reshape(CHUNK, width)
        slots = dot(spread[...], table[chunk][:, 0:128])
        number = 1.0
        for end in ends:
            number = number + (slots >= end).astype(F32)
        number = (number * diagonal).astype(BF16)
        cl_col[chunk] = dot(number, ones_col)
        cl_row[chunk] = dot_t(ones_row, number)

        def with_earlier(k, inner):
            chunk_k, v_k = chunk_of(k)

            @pl.when(v == core)
            def _():
                fold(chunk, chunk_k)

            @pl.when((v_k == core) & (k < w))
            def _():
                fold(chunk_k, chunk)

            return inner

        lax.fori_loop(0, w + 1, with_earlier, 0)
        return carry

    lax.fori_loop(0, WINDOWS, take_window, 0)

    slab_lane = quotient(iota((16, CHUNK), 1).astype(F32), SLAB)
    own_slab = slab_lane == iota((16, CHUNK), 0).astype(F32)
    fold_lanes = (diagonal > 0.5).astype(F32).astype(BF16)

    def give_back(u, carry):
        row = jnp.max(best[u], axis=0, keepdims=True)
        picked = jnp.where(own_slab, row, 0.0)
        table = sum(dot(piece, fold_lanes) for piece in thirds(picked))
        gone[pl.ds(pl.multiple_of(u * 16, 16), 16), :] = table

        def one(k, inner):
            sx, sy, sz = chip_of(u, core, k // 8, (k // 2) % 4)
            to = device_of(sx, sy, sz, k % 2)
            dx, dy, dz = (x0 - sx + 4) % 4, (y0 - sy + 4) % 4, (z0 - sz + 4) % 4
            du, dzx = (dy - dx + 4) % 4, (dz - dx + 4) % 4
            number = (du * 2 + dzx % 2) * 8 + (dzx // 2) * 4 + dx
            here = (to[0] * 4 + to[1]) == me

            @pl.when(jnp.logical_not(here))
            def _():
                pltpu.make_async_remote_copy(
                    src_ref=gone.at[pl.ds(u * 16 + k, 1)], dst_ref=back.at[pl.ds(number, 1)], send_sem=back_send_sem, recv_sem=back_sem,
                    device_id=to, device_id_type=MESH,
                ).start()

            @pl.when(here)
            def _():
                pltpu.make_async_copy(gone.at[pl.ds(u * 16 + k, 1)], back.at[pl.ds(number, 1)], back_sem).start()

            return inner

        lax.fori_loop(0, 16, one, 0)
        return carry

    lax.fori_loop(0, 4, give_back, 0)

    mine_too = v0 == core

    @pl.when(mine_too)
    def _():
        pltpu.make_async_copy(send.at[pl.ds(0, 63 * (SLAB // 8))], send.at[pl.ds(0, 63 * (SLAB // 8))], send_sem).wait()

    @pl.when(jnp.logical_not(mine_too))
    def _():
        pltpu.make_async_copy(send, send, send_sem).wait()

    def pass_sent(w, carry):
        chunk, v = chunk_of(w)

        @pl.when(v == core)
        def _():
            pass_copy(w, chunk).wait_send()

        return carry

    lax.fori_loop(0, WINDOWS, pass_sent, 0)

    pltpu.make_async_copy(back, back, back_sem).wait()
    result = jnp.full((1, row_count), -1.0, F32)
    got = jnp.concatenate([back[...], jnp.zeros((64, 128), F32)], axis=0).T
    pieces = thirds(got[:, 0:64])
    for k in range(2):
        hot_one = (slab_iota == picks[k:k + 1, :]).astype(F32).astype(BF16)
        table = sum(dot(piece, hot_one) for piece in pieces)
        mark = (lane_iota == ranks[k:k + 1, :]) & (picks[k:k + 1, :] >= 0)
        result = jnp.maximum(result, jnp.max(jnp.where(mark, table, -1.0), axis=0, keepdims=True))
    out_ref[...] = result

    @pl.when(v0 == core)
    def _():
        pltpu.make_async_copy(gone.at[pl.ds(0, 63)], gone.at[pl.ds(0, 63)], back_send_sem).wait()

    @pl.when(v0 != core)
    def _():
        pltpu.make_async_copy(gone, gone, back_send_sem).wait()


def on_device(embeddings, route, cluster):
    row_count, width = embeddings.shape
    vmem = pl.BlockSpec(memory_space=pltpu.VMEM)
    scores = pl.pallas_call(
        kernel,
        out_shape=jax.ShapeDtypeStruct((1, row_count), F32),
        in_specs=[vmem] * 3,
        out_specs=vmem,
        scratch_shapes=[
            pltpu.VMEM((row_count, width), BF16),
            pltpu.VMEM((8 * SLAB, 8, width), BF16),
            pltpu.VMEM((WINDOWS * CHUNK // 8, 8, width), BF16),
            pltpu.VMEM((WINDOWS, CHUNK, width), BF16),
            pltpu.VMEM((8, row_count), I32),
            pltpu.VMEM((8, row_count), I32),
            pltpu.VMEM((128, 128), BF16),
            pltpu.VMEM((8, 128), F32),
            pltpu.VMEM((3, 8, 128), F32),
            pltpu.VMEM((CHUNK, CHUNK), BF16),
            pltpu.VMEM((WINDOWS, CHUNK, 128), I32),
            pltpu.VMEM((WINDOWS, 8, CHUNK), I32),
            pltpu.VMEM((WINDOWS, CHUNK, 128), F32),
            pltpu.VMEM((WINDOWS, 8, CHUNK), F32),
            pltpu.VMEM((4, 8, CHUNK), F32),
            pltpu.VMEM((64, 128), F32),
            pltpu.VMEM((64, 128), F32),
            pltpu.SemaphoreType.DMA,
            pltpu.SemaphoreType.DMA((WINDOWS,)),
            pltpu.SemaphoreType.DMA((WINDOWS,)),
            pltpu.SemaphoreType.DMA((WINDOWS,)),
            pltpu.SemaphoreType.DMA((3,)),
            pltpu.SemaphoreType.DMA((3,)),
            pltpu.SemaphoreType.DMA,
            pltpu.SemaphoreType.DMA,
        ],
        compiler_params=pltpu.CompilerParams(collective_id=0, has_side_effects=True, vmem_limit_bytes=56 * 1024 * 1024),
    )(embeddings, route.reshape(1, row_count), cluster)
    return scores.reshape(row_count)


def solution(mesh):
    in_specs = (P(("grp", "blk"), None), P(("grp", "blk")), P("grp", "blk"))
    return jax.shard_map(on_device, mesh=mesh, in_specs=in_specs, out_specs=P(("grp", "blk")), check_vma=False)
```

```python
import functools

import jax
import jax.numpy as jnp
from jax import lax
from jax.experimental import pallas as pl
from jax.experimental.pallas import tpu as pltpu
from jax.sharding import PartitionSpec as P

MESH = pl.DeviceIdType.MESH
F32, BF16, I32 = jnp.float32, jnp.bfloat16, jnp.int32
SLAB = 40
USED = 36
WINDOWS = 8
CHUNK = 16 * SLAB


def dot(a, b):
    return lax.dot_general(a, b, (((1,), (0,)), ((), ())), preferred_element_type=F32)


def dot_t(a, b):
    return lax.dot_general(a, b, (((1,), (1,)), ((), ())), preferred_element_type=F32)


def iota(shape, dim):
    return lax.broadcasted_iota(I32, shape, dim)


def quotient(value, by):
    return jnp.floor((value + 0.5) * (1.0 / by))


def thirds(value):
    first = value.astype(BF16)
    rest = value - first.astype(F32)
    second = rest.astype(BF16)
    return first, second, (rest - second.astype(F32)).astype(BF16)


def window_shift(w):
    return (7 - w) // 2, (7 - w) % 2


def chip_of(u, v, e, x):
    return x, (u + x) % 4, (v + 2 * e + x) % 4


def device_of(x, y, z, core):
    return (y % 2) * 16 + z * 4 + x, (y // 2) * 2 + core


def kernel(
    emb_ref, route_ref, cluster_ref, out_ref,
    unit, send, rows, table, picks, ranks, meta, count, counts, spread, key_col, key_row, cl_col, cl_row, best, best_t, gone, back,
    send_sem, recv_sem, pass_sem, pass_send_sem, count_sem, count_send_sem, back_sem, back_send_sem,
):
    row_count, width = emb_ref.shape
    grp, blk = lax.axis_index("grp"), lax.axis_index("blk")
    me = grp * 4 + blk
    y_lo, z0, x0 = grp // 16, (grp // 4) % 4, grp % 4
    y0, core = (blk // 2) * 2 + y_lo, blk % 2
    u0, v0, e0 = (y0 - x0 + 4) % 4, (z0 - x0 + 4) % 2, ((z0 - x0 + 4) % 4) // 2
    sibling = (grp, blk + 1 - 2 * core)

    barrier = pltpu.get_barrier_semaphore()

    def greet(i, carry):
        other = (me + 1 + i) % 128
        pl.semaphore_signal(barrier, inc=1, device_id=(other // 4, other % 4), device_id_type=MESH)
        return carry

    lax.fori_loop(0, 127, greet, 0)

    values = emb_ref[...].astype(F32)
    unit[...] = (values * lax.rsqrt(jnp.sum(values * values, axis=1, keepdims=True) + 1e-06)).astype(BF16)

    route = jnp.concatenate([route_ref[k:k + 1, :] for k in range(row_count // 128)], axis=1).astype(F32)
    family = quotient(route, 6144)
    slot = route - family * 6144
    block = quotient(slot, 1536)
    slot_hi = quotient(slot, 48)
    slot_lo = slot - slot_hi * 48
    family_int = family.astype(I32)
    fam_y, fam_z, fam_x = family_int >> 4, (family_int >> 2) & 3, family_int & 3

    def order_number(y):
        dx, dy, dz = (fam_x - x0) & 3, (y - y0) & 3, (fam_z - z0) & 3
        du, dzx = (dy - dx) & 3, (dz - dx) & 3
        return (7 - du * 2 - (dzx & 1)) * 8 + (1 - (dzx >> 1)) * 4 + 3 - dx

    pick_a = jnp.where(block < 2.5, order_number(fam_y), -1)
    pick_b = jnp.where(block > 0.5, order_number(fam_y + 2), -1)
    slab_iota = iota((64, row_count), 0)
    hot_a = (slab_iota == pick_a).astype(F32)
    hot_b = (slab_iota == pick_b).astype(F32)
    hot = (hot_a + hot_b).astype(BF16)
    earlier = (iota((256, 256), 0) < iota((256, 256), 1)).astype(F32).astype(BF16)
    before = jnp.zeros((64, 1), F32)
    prefix = []
    for k in range(row_count // 256):
        part = hot[:, k * 256:(k + 1) * 256]
        prefix.append(dot(part, earlier) + before)
        before = before + jnp.sum(part.astype(F32), axis=1, keepdims=True)
    prefix = jnp.concatenate(prefix, axis=1)
    rank_a = jnp.sum(hot_a * prefix, axis=0, keepdims=True).astype(I32)
    rank_b = jnp.sum(hot_b * prefix, axis=0, keepdims=True).astype(I32)
    picks[0:1, :], picks[1:2, :] = pick_a, pick_b
    ranks[0:1, :], ranks[1:2, :] = rank_a, rank_b
    lane_iota = iota((128, row_count), 0)
    hi = jnp.zeros((64, 128), F32)
    lo = jnp.zeros((64, 128), F32)
    for hot_one, rank in ((hot_a, rank_a), (hot_b, rank_b)):
        chosen = lane_iota == rank
        hi = hi + dot_t(hot_one.astype(BF16), jnp.where(chosen, slot_hi, 0.0).astype(BF16))
        lo = lo + dot_t(hot_one.astype(BF16), jnp.where(chosen, slot_lo, 0.0).astype(BF16))
    meta[0:64, :] = hi.astype(BF16)
    meta[64:128, :] = lo.astype(BF16)

    cluster = cluster_ref[...]
    which = iota((8, 128), 0)
    tally = jnp.zeros((8, 128), F32)
    for k in range(1, 4):
        below = jnp.sum((cluster < k).astype(F32), axis=1, keepdims=True)
        tally = jnp.where(which == k, below, tally)
    count[...] = tally

    pl.semaphore_wait(barrier, 127)

    def count_copy(step):
        return pltpu.make_async_remote_copy(
            src_ref=count, dst_ref=counts.at[step], send_sem=count_send_sem.at[step], recv_sem=count_sem.at[step],
            device_id=(grp, (blk + 1 + step) % 4), device_id_type=MESH,
        )

    for step in range(3):
        count_copy(step).start()

    target_a = jnp.where(pick_a >= 0, pick_a * SLAB + rank_a, -1)
    target_b = jnp.where(pick_b >= 0, pick_b * SLAB + rank_b, -1)
    picks[2:3, :], picks[3:4, :] = target_a, target_b
    home_row = ((v0 * 4 + u0) * 16 + (e0 * 4 + x0) * 2 + core) * (SLAB // 8)
    p_col = iota((8 * SLAB, 128), 0).astype(F32)
    p_slab = quotient(p_col, SLAB)
    p_in = (p_col - p_slab * SLAB).astype(I32)
    p_slab = p_slab.astype(I32)
    p_lane = iota((8 * SLAB, 128), 1)

    def make_window(w, carry):
        p_iota = iota((8 * SLAB, row_count), 0) + w * (8 * SLAB)
        one_hot = ((p_iota == picks[2:3, :]) | (p_iota == picks[3:4, :])).astype(F32).astype(BF16)
        body = dot(one_hot, unit[...])
        slab_no = p_slab + w * 8
        info_hot = (((p_in == USED) & (p_lane == slab_no)) | ((p_in == USED + 1) & (p_lane == slab_no + 64))).astype(F32).astype(BF16)
        info = dot(info_hot, meta[...])
        base = w * SLAB
        body = jnp.concatenate([body[:, 0:128] + info, body[:, 128:width]], axis=1).astype(BF16)
        send[pl.ds(base, SLAB)] = body.reshape(SLAB, 8, width)
        du, dv = window_shift(w)

        def send_one(k, inner):
            dx, dy, dz = chip_of(du, dv, 1 - k // 4, 3 - k % 4)
            to = device_of((x0 + dx) % 4, (y0 + dy) % 4, (z0 + dz) % 4, v0)
            source = send.at[pl.ds((w * 8 + k) * (SLAB // 8), SLAB // 8)]
            here = (to[0] * 4 + to[1]) == me

            @pl.when(jnp.logical_not(here))
            def _():
                pltpu.make_async_remote_copy(
                    src_ref=source, dst_ref=rows.at[pl.ds(home_row, SLAB // 8)], send_sem=send_sem, recv_sem=recv_sem.at[w],
                    device_id=to, device_id_type=MESH,
                ).start()

            @pl.when(here)
            def _():
                pltpu.make_async_copy(source, rows.at[pl.ds(home_row, SLAB // 8)], recv_sem.at[w]).start()

            return inner

        lax.fori_loop(0, 8, send_one, 0)
        return carry

    lax.fori_loop(0, WINDOWS, make_window, 0)

    p = iota((CHUNK, 128), 0).astype(F32)
    slab_of = quotient(p, SLAB)
    in_slab = p - slab_of * SLAB
    diagonal = ((iota((CHUNK, 128), 1).astype(F32) == in_slab) & (in_slab < USED)).astype(F32)
    other = iota((CHUNK, CHUNK), 1).astype(F32)
    p_wide = iota((CHUNK, CHUNK), 0).astype(F32)
    first = quotient(p_wide, SLAB) * SLAB
    spread[...] = jnp.where(other == first + USED, 48.0, jnp.where(other == first + (USED + 1), 1.0, 0.0)).astype(BF16)

    def data_key(slab_no, inside, u, v):
        sx, se, sc = (slab_no >> 1) & 3, slab_no >> 3, slab_no & 1
        sy, sz = (u + sx) & 3, (v + 2 * se + sx) & 3
        source = ((sy & 1) * 16 + sz * 4 + sx) * 4 + (sy >> 1) * 2 + sc
        return source * SLAB + inside

    slab_col, in_col = slab_of.astype(I32), in_slab.astype(I32)
    q = iota((8, CHUNK), 1).astype(F32)
    slab_row = quotient(q, SLAB)
    in_row = (q - slab_row * SLAB).astype(I32)
    slab_row = slab_row.astype(I32)

    def make_keys(k, carry):
        key_col[k] = data_key(slab_col, in_col, k % 4, k // 4)
        key_row[k] = data_key(slab_row, in_row, k % 4, k // 4)
        return carry

    lax.fori_loop(0, WINDOWS, make_keys, 0)
    best[...] = jnp.full(best.shape, -1.0, F32)
    best_t[...] = jnp.full(best_t.shape, -1.0, F32)

    total = count[...]
    for step in range(3):
        count_copy(step).wait()
        total = total + counts[step]
    ends = [total[k:k + 1, :] for k in range(1, 4)]
    ones_col = jnp.ones((128, 128), BF16)
    ones_row = jnp.ones((8, 128), BF16)

    def chunk_of(w):
        du, dv = window_shift(w)
        u, v = (u0 - du + 4) % 4, (v0 - dv + 2) % 2
        return v * 4 + u, v

    def pass_copy(w, chunk):
        part = rows.at[pl.ds(chunk * (CHUNK // 8), CHUNK // 8)]
        return pltpu.make_async_remote_copy(
            src_ref=part, dst_ref=part, send_sem=pass_send_sem.at[w], recv_sem=pass_sem.at[w],
            device_id=sibling, device_id_type=MESH,
        )

    def fold(mine, others, both=False):
        x_mine = table[mine]
        x_other = table[others]
        scores = dot_t(x_other, x_mine)
        wide = lambda a: jnp.concatenate([a] * (CHUNK // 128), axis=1)
        same = wide(cl_col[others]) == cl_row[mine][0:1, :]
        prior = wide(key_col[others]) < key_row[mine][0:1, :]
        held = jnp.where(same & prior, scores, -1.0).reshape(CHUNK // 8, 8, CHUNK)
        u = mine % 4
        best[u] = jnp.maximum(best[u], jnp.max(held, axis=0))
        if both:
            later = jnp.where(same & jnp.logical_not(prior), scores, -1.0)
            most = later[:, 0:128]
            for k in range(1, CHUNK // 128):
                most = jnp.maximum(most, later[:, k * 128:(k + 1) * 128])
            t = others % 4
            best_t[t] = jnp.maximum(best_t[t], most)

    def take_window(w, carry):
        chunk, v = chunk_of(w)
        part = rows.at[pl.ds(chunk * (CHUNK // 8), CHUNK // 8)]

        @pl.when(v == core)
        def _():
            pltpu.make_async_copy(part, part, recv_sem.at[w]).wait()
            pass_copy(w, chunk).start()

        @pl.when(v != core)
        def _():
            pltpu.make_async_copy(part, part, pass_sem.at[w]).wait()

        table[chunk] = rows[pl.ds(chunk * (CHUNK // 8), CHUNK // 8)].reshape(CHUNK, width)
        slots = dot(spread[...], table[chunk][:, 0:128])
        number = 1.0
        for end in ends:
            number = number + (slots >= end).astype(F32)
        number = (number * diagonal).astype(BF16)
        cl_col[chunk] = dot(number, ones_col)
        cl_row[chunk] = dot_t(ones_row, number)

        def with_earlier(k, inner):
            chunk_k, v_k = chunk_of(k)

            @pl.when((v == core) & ((v_k != core) | (k == w)))
            def _():
                fold(chunk, chunk_k)

            @pl.when((v == core) & (v_k == core) & (k < w))
            def _():
                fold(chunk, chunk_k, both=True)

            @pl.when((v != core) & (v_k == core))
            def _():
                fold(chunk_k, chunk)

            return inner

        lax.fori_loop(0, w + 1, with_earlier, 0)
        return carry

    lax.fori_loop(0, WINDOWS, take_window, 0)

    slab_lane = quotient(iota((16, CHUNK), 1).astype(F32), SLAB)
    own_slab = slab_lane == iota((16, CHUNK), 0).astype(F32)
    as_slabs = own_slab.astype(F32).astype(BF16)
    fold_lanes = (diagonal > 0.5).astype(F32).astype(BF16)

    def give_back(u, carry):
        row = jnp.max(best[u], axis=0, keepdims=True)
        picked = jnp.where(own_slab, row, 0.0)
        table = sum(dot(piece, fold_lanes) for piece in thirds(picked))
        listed = jnp.where(diagonal > 0.5, jnp.max(best_t[u], axis=1, keepdims=True), 0.0)
        table_t = sum(dot(as_slabs, piece) for piece in thirds(listed))
        gone[pl.ds(pl.multiple_of(u * 16, 16), 16), :] = jnp.maximum(table, table_t)

        def one(k, inner):
            sx, sy, sz = chip_of(u, core, k // 8, (k // 2) % 4)
            to = device_of(sx, sy, sz, k % 2)
            dx, dy, dz = (x0 - sx + 4) % 4, (y0 - sy + 4) % 4, (z0 - sz + 4) % 4
            du, dzx = (dy - dx + 4) % 4, (dz - dx + 4) % 4
            number = (7 - du * 2 - dzx % 2) * 8 + (1 - dzx // 2) * 4 + 3 - dx
            here = (to[0] * 4 + to[1]) == me

            @pl.when(jnp.logical_not(here))
            def _():
                pltpu.make_async_remote_copy(
                    src_ref=gone.at[pl.ds(u * 16 + k, 1)], dst_ref=back.at[pl.ds(number, 1)], send_sem=back_send_sem, recv_sem=back_sem,
                    device_id=to, device_id_type=MESH,
                ).start()

            @pl.when(here)
            def _():
                pltpu.make_async_copy(gone.at[pl.ds(u * 16 + k, 1)], back.at[pl.ds(number, 1)], back_sem).start()

            return inner

        lax.fori_loop(0, 16, one, 0)
        return carry

    lax.fori_loop(0, 4, give_back, 0)

    mine_too = v0 == core

    @pl.when(mine_too)
    def _():
        pltpu.make_async_copy(send.at[pl.ds(0, 63 * (SLAB // 8))], send.at[pl.ds(0, 63 * (SLAB // 8))], send_sem).wait()

    @pl.when(jnp.logical_not(mine_too))
    def _():
        pltpu.make_async_copy(send, send, send_sem).wait()

    def pass_sent(w, carry):
        chunk, v = chunk_of(w)

        @pl.when(v == core)
        def _():
            pass_copy(w, chunk).wait_send()

        return carry

    lax.fori_loop(0, WINDOWS, pass_sent, 0)

    pltpu.make_async_copy(back, back, back_sem).wait()
    result = jnp.full((1, row_count), -1.0, F32)
    got = jnp.concatenate([back[...], jnp.zeros((64, 128), F32)], axis=0).T
    pieces = thirds(got[:, 0:64])
    for k in range(2):
        hot_one = (slab_iota == picks[k:k + 1, :]).astype(F32).astype(BF16)
        table = sum(dot(piece, hot_one) for piece in pieces)
        mark = (lane_iota == ranks[k:k + 1, :]) & (picks[k:k + 1, :] >= 0)
        result = jnp.maximum(result, jnp.max(jnp.where(mark, table, -1.0), axis=0, keepdims=True))
    for k in range(row_count // 128):
        out_ref[k:k + 1, :] = result[:, k * 128:(k + 1) * 128]

    @pl.when(v0 == core)
    def _():
        pltpu.make_async_copy(gone.at[pl.ds(0, 63)], gone.at[pl.ds(0, 63)], back_send_sem).wait()

    @pl.when(v0 != core)
    def _():
        pltpu.make_async_copy(gone, gone, back_send_sem).wait()


def on_device(embeddings, route, cluster):
    row_count, width = embeddings.shape
    vmem = pl.BlockSpec(memory_space=pltpu.VMEM)
    scores = pl.pallas_call(
        kernel,
        out_shape=jax.ShapeDtypeStruct((row_count // 128, 128), F32),
        in_specs=[vmem] * 3,
        out_specs=vmem,
        scratch_shapes=[
            pltpu.VMEM((row_count, width), BF16),
            pltpu.VMEM((8 * SLAB, 8, width), BF16),
            pltpu.VMEM((WINDOWS * CHUNK // 8, 8, width), BF16),
            pltpu.VMEM((WINDOWS, CHUNK, width), BF16),
            pltpu.VMEM((8, row_count), I32),
            pltpu.VMEM((8, row_count), I32),
            pltpu.VMEM((128, 128), BF16),
            pltpu.VMEM((8, 128), F32),
            pltpu.VMEM((3, 8, 128), F32),
            pltpu.VMEM((CHUNK, CHUNK), BF16),
            pltpu.VMEM((WINDOWS, CHUNK, 128), I32),
            pltpu.VMEM((WINDOWS, 8, CHUNK), I32),
            pltpu.VMEM((WINDOWS, CHUNK, 128), F32),
            pltpu.VMEM((WINDOWS, 8, CHUNK), F32),
            pltpu.VMEM((4, 8, CHUNK), F32),
            pltpu.VMEM((4, CHUNK, 128), F32),
            pltpu.VMEM((64, 128), F32),
            pltpu.VMEM((64, 128), F32),
            pltpu.SemaphoreType.DMA,
            pltpu.SemaphoreType.DMA((WINDOWS,)),
            pltpu.SemaphoreType.DMA((WINDOWS,)),
            pltpu.SemaphoreType.DMA((WINDOWS,)),
            pltpu.SemaphoreType.DMA((3,)),
            pltpu.SemaphoreType.DMA((3,)),
            pltpu.SemaphoreType.DMA,
            pltpu.SemaphoreType.DMA,
        ],
        compiler_params=pltpu.CompilerParams(collective_id=0, has_side_effects=True, vmem_limit_bytes=56 * 1024 * 1024),
    )(embeddings, route.reshape(row_count // 128, 128), cluster)
    return scores.reshape(row_count)


def solution(mesh):
    in_specs = (P(("grp", "blk"), None), P(("grp", "blk")), P("grp", "blk"))
    return jax.shard_map(on_device, mesh=mesh, in_specs=in_specs, out_specs=P(("grp", "blk")), check_vma=False)
```

```python
import functools

import jax
import jax.numpy as jnp
from jax import lax
from jax.experimental import pallas as pl
from jax.experimental.pallas import tpu as pltpu
from jax.sharding import PartitionSpec as P

MESH = pl.DeviceIdType.MESH
F32, BF16, I32 = jnp.float32, jnp.bfloat16, jnp.int32
SLAB = 40
USED = 36
WINDOWS = 8
CHUNK = 16 * SLAB


def dot(a, b):
    return lax.dot_general(a, b, (((1,), (0,)), ((), ())), preferred_element_type=F32)


def dot_t(a, b):
    return lax.dot_general(a, b, (((1,), (1,)), ((), ())), preferred_element_type=F32)


def iota(shape, dim):
    return lax.broadcasted_iota(I32, shape, dim)


def quotient(value, by):
    return jnp.floor((value + 0.5) * (1.0 / by))


def thirds(value):
    first = value.astype(BF16)
    rest = value - first.astype(F32)
    second = rest.astype(BF16)
    return first, second, (rest - second.astype(F32)).astype(BF16)


def window_shift(w):
    return (7 - w) // 2, (7 - w) % 2


def chip_of(u, v, e, x):
    return x, (u + x) % 4, (v + 2 * e + x) % 4


def device_of(x, y, z, core):
    return (y % 2) * 16 + z * 4 + x, (y // 2) * 2 + core


def kernel(
    emb_ref, route_ref, cluster_ref, out_ref,
    unit, send, rows, table, picks, ranks, meta, count, counts, spread, key_col, key_row, cl_col, cl_row, best, best_t, gone, back,
    send_sem, recv_sem, pass_sem, pass_send_sem, count_sem, count_send_sem, back_sem, back_send_sem,
):
    row_count, width = emb_ref.shape
    grp, blk = lax.axis_index("grp"), lax.axis_index("blk")
    me = grp * 4 + blk
    y_lo, z0, x0 = grp // 16, (grp // 4) % 4, grp % 4
    y0, core = (blk // 2) * 2 + y_lo, blk % 2
    u0, v0, e0 = (y0 - x0 + 4) % 4, (z0 - x0 + 4) % 2, ((z0 - x0 + 4) % 4) // 2
    sibling = (grp, blk + 1 - 2 * core)

    barrier = pltpu.get_barrier_semaphore()

    def greet(i, carry):
        other = ((me >> 1) + 1 + i) & 63
        pl.semaphore_signal(barrier, inc=1, device_id=(other >> 1, (other & 1) * 2 + v0), device_id_type=MESH)
        return carry

    def greet_more(i, carry):
        x = i & 3
        to = device_of(x, (i >> 2) & 3, (i >> 4) * 2 + ((core + x) & 1), 1 - v0)
        pl.semaphore_signal(barrier, inc=1, device_id=to, device_id_type=MESH)
        return carry

    lax.fori_loop(0, jnp.where(v0 == core, 63, 64), greet, 0)
    lax.fori_loop(0, 32, greet_more, 0)

    @pl.when(v0 != core)
    def _():
        pl.semaphore_signal(barrier, inc=1, device_id=(grp, (blk + 2) % 4), device_id_type=MESH)

    values = emb_ref[...].astype(F32)
    unit[...] = (values * lax.rsqrt(jnp.sum(values * values, axis=1, keepdims=True) + 1e-06)).astype(BF16)

    route = jnp.concatenate([route_ref[k:k + 1, :] for k in range(row_count // 128)], axis=1).astype(F32)
    family = quotient(route, 6144)
    slot = route - family * 6144
    block = quotient(slot, 1536)
    slot_hi = quotient(slot, 48)
    slot_lo = slot - slot_hi * 48
    family_int = family.astype(I32)
    fam_y, fam_z, fam_x = family_int >> 4, (family_int >> 2) & 3, family_int & 3

    def order_number(y):
        dx, dy, dz = (fam_x - x0) & 3, (y - y0) & 3, (fam_z - z0) & 3
        du, dzx = (dy - dx) & 3, (dz - dx) & 3
        return (7 - du * 2 - (dzx & 1)) * 8 + (1 - (dzx >> 1)) * 4 + 3 - dx

    pick_a = jnp.where(block < 2.5, order_number(fam_y), -1)
    pick_b = jnp.where(block > 0.5, order_number(fam_y + 2), -1)
    slab_iota = iota((64, row_count), 0)
    hot_a = (slab_iota == pick_a).astype(F32)
    hot_b = (slab_iota == pick_b).astype(F32)
    hot = (hot_a + hot_b).astype(BF16)
    earlier = (iota((256, 256), 0) < iota((256, 256), 1)).astype(F32).astype(BF16)
    before = jnp.zeros((64, 1), F32)
    prefix = []
    for k in range(row_count // 256):
        part = hot[:, k * 256:(k + 1) * 256]
        prefix.append(dot(part, earlier) + before)
        before = before + jnp.sum(part.astype(F32), axis=1, keepdims=True)
    prefix = jnp.concatenate(prefix, axis=1)
    rank_a = jnp.sum(hot_a * prefix, axis=0, keepdims=True).astype(I32)
    rank_b = jnp.sum(hot_b * prefix, axis=0, keepdims=True).astype(I32)
    picks[0:1, :], picks[1:2, :] = pick_a, pick_b
    ranks[0:1, :], ranks[1:2, :] = rank_a, rank_b
    lane_iota = iota((128, row_count), 0)
    hi = jnp.zeros((64, 128), F32)
    lo = jnp.zeros((64, 128), F32)
    for hot_one, rank in ((hot_a, rank_a), (hot_b, rank_b)):
        chosen = lane_iota == rank
        hi = hi + dot_t(hot_one.astype(BF16), jnp.where(chosen, slot_hi, 0.0).astype(BF16))
        lo = lo + dot_t(hot_one.astype(BF16), jnp.where(chosen, slot_lo, 0.0).astype(BF16))
    meta[0:64, :] = hi.astype(BF16)
    meta[64:128, :] = lo.astype(BF16)

    cluster = cluster_ref[...]
    which = iota((8, 128), 0)
    tally = jnp.zeros((8, 128), F32)
    for k in range(1, 4):
        below = jnp.sum((cluster < k).astype(F32), axis=1, keepdims=True)
        tally = jnp.where(which == k, below, tally)
    count[...] = tally

    @pl.when(v0 == core)
    def _():
        pl.semaphore_wait(barrier, 95)

    @pl.when(v0 != core)
    def _():
        pl.semaphore_wait(barrier, 97)

    def count_copy(step):
        return pltpu.make_async_remote_copy(
            src_ref=count, dst_ref=counts.at[step], send_sem=count_send_sem.at[step], recv_sem=count_sem.at[step],
            device_id=(grp, (blk + 1 + step) % 4), device_id_type=MESH,
        )

    for step in range(3):
        count_copy(step).start()

    target_a = jnp.where(pick_a >= 0, pick_a * SLAB + rank_a, -1)
    target_b = jnp.where(pick_b >= 0, pick_b * SLAB + rank_b, -1)
    picks[2:3, :], picks[3:4, :] = target_a, target_b
    home_row = ((v0 * 4 + u0) * 16 + (e0 * 4 + x0) * 2 + core) * (SLAB // 8)
    p_col = iota((8 * SLAB, 128), 0).astype(F32)
    p_slab = quotient(p_col, SLAB)
    p_in = (p_col - p_slab * SLAB).astype(I32)
    p_slab = p_slab.astype(I32)
    p_lane = iota((8 * SLAB, 128), 1)

    def make_window(w, carry):
        p_iota = iota((8 * SLAB, row_count), 0) + w * (8 * SLAB)
        one_hot = ((p_iota == picks[2:3, :]) | (p_iota == picks[3:4, :])).astype(F32).astype(BF16)
        body = dot(one_hot, unit[...])
        slab_no = p_slab + w * 8
        info_hot = (((p_in == USED) & (p_lane == slab_no)) | ((p_in == USED + 1) & (p_lane == slab_no + 64))).astype(F32).astype(BF16)
        info = dot(info_hot, meta[...])
        base = w * SLAB
        body = jnp.concatenate([body[:, 0:128] + info, body[:, 128:width]], axis=1).astype(BF16)
        send[pl.ds(base, SLAB)] = body.reshape(SLAB, 8, width)
        du, dv = window_shift(w)

        def send_one(k, inner):
            dx, dy, dz = chip_of(du, dv, 1 - k // 4, 3 - k % 4)
            to = device_of((x0 + dx) % 4, (y0 + dy) % 4, (z0 + dz) % 4, v0)
            source = send.at[pl.ds((w * 8 + k) * (SLAB // 8), SLAB // 8)]
            here = (to[0] * 4 + to[1]) == me

            @pl.when(jnp.logical_not(here))
            def _():
                pltpu.make_async_remote_copy(
                    src_ref=source, dst_ref=rows.at[pl.ds(home_row, SLAB // 8)], send_sem=send_sem, recv_sem=recv_sem.at[w],
                    device_id=to, device_id_type=MESH,
                ).start()

            @pl.when(here)
            def _():
                pltpu.make_async_copy(source, rows.at[pl.ds(home_row, SLAB // 8)], recv_sem.at[w]).start()

            return inner

        lax.fori_loop(0, 8, send_one, 0, unroll=2)
        return carry

    lax.fori_loop(0, WINDOWS, make_window, 0)

    p = iota((CHUNK, 128), 0).astype(F32)
    slab_of = quotient(p, SLAB)
    in_slab = p - slab_of * SLAB
    diagonal = ((iota((CHUNK, 128), 1).astype(F32) == in_slab) & (in_slab < USED)).astype(F32)
    other = iota((CHUNK, CHUNK), 1).astype(F32)
    p_wide = iota((CHUNK, CHUNK), 0).astype(F32)
    first = quotient(p_wide, SLAB) * SLAB
    spread[...] = jnp.where(other == first + USED, 48.0, jnp.where(other == first + (USED + 1), 1.0, 0.0)).astype(BF16)

    def data_key(slab_no, inside, u, v):
        sx, se, sc = (slab_no >> 1) & 3, slab_no >> 3, slab_no & 1
        sy, sz = (u + sx) & 3, (v + 2 * se + sx) & 3
        source = ((sy & 1) * 16 + sz * 4 + sx) * 4 + (sy >> 1) * 2 + sc
        return source * SLAB + inside

    slab_col, in_col = slab_of.astype(I32), in_slab.astype(I32)
    q = iota((8, CHUNK), 1).astype(F32)
    slab_row = quotient(q, SLAB)
    in_row = (q - slab_row * SLAB).astype(I32)
    slab_row = slab_row.astype(I32)

    def make_keys(k, carry):
        key_col[k] = data_key(slab_col, in_col, k % 4, k // 4)
        key_row[k] = data_key(slab_row, in_row, k % 4, k // 4)
        return carry

    lax.fori_loop(0, WINDOWS, make_keys, 0)
    best[...] = jnp.full(best.shape, -1.0, F32)
    best_t[...] = jnp.full(best_t.shape, -1.0, F32)

    total = count[...]
    for step in range(3):
        count_copy(step).wait()
        total = total + counts[step]
    ends = [total[k:k + 1, :] for k in range(1, 4)]
    ones_col = jnp.ones((128, 128), BF16)
    ones_row = jnp.ones((8, 128), BF16)

    def chunk_of(w):
        du, dv = window_shift(w)
        u, v = (u0 - du + 4) % 4, (v0 - dv + 2) % 2
        return v * 4 + u, v

    def pass_copy(w, chunk):
        part = rows.at[pl.ds(chunk * (CHUNK // 8), CHUNK // 8)]
        return pltpu.make_async_remote_copy(
            src_ref=part, dst_ref=part, send_sem=pass_send_sem.at[w], recv_sem=pass_sem.at[w],
            device_id=sibling, device_id_type=MESH,
        )

    def fold(mine, others, both=False):
        x_mine = table[mine]
        x_other = table[others]
        scores = dot_t(x_other, x_mine)
        wide = lambda a: jnp.concatenate([a] * (CHUNK // 128), axis=1)
        same = wide(cl_col[others]) == cl_row[mine][0:1, :]
        prior = wide(key_col[others]) < key_row[mine][0:1, :]
        held = jnp.where(same & prior, scores, -1.0).reshape(CHUNK // 8, 8, CHUNK)
        u = mine % 4
        best[u] = jnp.maximum(best[u], jnp.max(held, axis=0))
        if both:
            later = jnp.where(same & jnp.logical_not(prior), scores, -1.0)
            most = later[:, 0:128]
            for k in range(1, CHUNK // 128):
                most = jnp.maximum(most, later[:, k * 128:(k + 1) * 128])
            t = others % 4
            best_t[t] = jnp.maximum(best_t[t], most)

    def take_window(w, carry):
        chunk, v = chunk_of(w)
        part = rows.at[pl.ds(chunk * (CHUNK // 8), CHUNK // 8)]

        @pl.when(v == core)
        def _():
            pltpu.make_async_copy(part, part, recv_sem.at[w]).wait()
            pass_copy(w, chunk).start()

        @pl.when(v != core)
        def _():
            pltpu.make_async_copy(part, part, pass_sem.at[w]).wait()

        table[chunk] = rows[pl.ds(chunk * (CHUNK // 8), CHUNK // 8)].reshape(CHUNK, width)
        slots = dot(spread[...], table[chunk][:, 0:128])
        number = 1.0
        for end in ends:
            number = number + (slots >= end).astype(F32)
        number = (number * diagonal).astype(BF16)
        cl_col[chunk] = dot(number, ones_col)
        cl_row[chunk] = dot_t(ones_row, number)

        def with_earlier(k, inner):
            chunk_k, v_k = chunk_of(k)

            @pl.when((v == core) & ((v_k != core) | (k == w)))
            def _():
                fold(chunk, chunk_k)

            @pl.when((v == core) & (v_k == core) & (k < w))
            def _():
                fold(chunk, chunk_k, both=True)

            @pl.when((v != core) & (v_k == core))
            def _():
                fold(chunk_k, chunk)

            return inner

        lax.fori_loop(0, w + 1, with_earlier, 0)
        return carry

    lax.fori_loop(0, WINDOWS, take_window, 0)

    slab_lane = quotient(iota((16, CHUNK), 1).astype(F32), SLAB)
    own_slab = slab_lane == iota((16, CHUNK), 0).astype(F32)
    as_slabs = own_slab.astype(F32).astype(BF16)
    fold_lanes = (diagonal > 0.5).astype(F32).astype(BF16)

    def give_back(u, carry):
        row = jnp.max(best[u], axis=0, keepdims=True)
        picked = jnp.where(own_slab, row, 0.0)
        table = sum(dot(piece, fold_lanes) for piece in thirds(picked))
        listed = jnp.where(diagonal > 0.5, jnp.max(best_t[u], axis=1, keepdims=True), 0.0)
        table_t = sum(dot(as_slabs, piece) for piece in thirds(listed))
        gone[pl.ds(pl.multiple_of(u * 16, 16), 16), :] = jnp.maximum(table, table_t)

        def one(k, inner):
            sx, sy, sz = chip_of(u, core, k // 8, (k // 2) % 4)
            to = device_of(sx, sy, sz, k % 2)
            dx, dy, dz = (x0 - sx + 4) % 4, (y0 - sy + 4) % 4, (z0 - sz + 4) % 4
            du, dzx = (dy - dx + 4) % 4, (dz - dx + 4) % 4
            number = (7 - du * 2 - dzx % 2) * 8 + (1 - dzx // 2) * 4 + 3 - dx
            here = (to[0] * 4 + to[1]) == me

            @pl.when(jnp.logical_not(here))
            def _():
                pltpu.make_async_remote_copy(
                    src_ref=gone.at[pl.ds(u * 16 + k, 1)], dst_ref=back.at[pl.ds(number, 1)], send_sem=back_send_sem, recv_sem=back_sem,
                    device_id=to, device_id_type=MESH,
                ).start()

            @pl.when(here)
            def _():
                pltpu.make_async_copy(gone.at[pl.ds(u * 16 + k, 1)], back.at[pl.ds(number, 1)], back_sem).start()

            return inner

        lax.fori_loop(0, 16, one, 0, unroll=4)
        return carry

    lax.fori_loop(0, 4, give_back, 0)

    mine_too = v0 == core

    @pl.when(mine_too)
    def _():
        pltpu.make_async_copy(send.at[pl.ds(0, 63 * (SLAB // 8))], send.at[pl.ds(0, 63 * (SLAB // 8))], send_sem).wait()

    @pl.when(jnp.logical_not(mine_too))
    def _():
        pltpu.make_async_copy(send, send, send_sem).wait()

    def pass_sent(w, carry):
        chunk, v = chunk_of(w)

        @pl.when(v == core)
        def _():
            pass_copy(w, chunk).wait_send()

        return carry

    lax.fori_loop(0, WINDOWS, pass_sent, 0)

    pltpu.make_async_copy(back, back, back_sem).wait()
    result = jnp.full((1, row_count), -1.0, F32)
    got = jnp.concatenate([back[...], jnp.zeros((64, 128), F32)], axis=0).T
    pieces = thirds(got[:, 0:64])
    for k in range(2):
        hot_one = (slab_iota == picks[k:k + 1, :]).astype(F32).astype(BF16)
        table = sum(dot(piece, hot_one) for piece in pieces)
        mark = (lane_iota == ranks[k:k + 1, :]) & (picks[k:k + 1, :] >= 0)
        result = jnp.maximum(result, jnp.max(jnp.where(mark, table, -1.0), axis=0, keepdims=True))
    for k in range(row_count // 128):
        out_ref[k:k + 1, :] = result[:, k * 128:(k + 1) * 128]

    @pl.when(v0 == core)
    def _():
        pltpu.make_async_copy(gone.at[pl.ds(0, 63)], gone.at[pl.ds(0, 63)], back_send_sem).wait()

    @pl.when(v0 != core)
    def _():
        pltpu.make_async_copy(gone, gone, back_send_sem).wait()


def on_device(embeddings, route, cluster):
    row_count, width = embeddings.shape
    vmem = pl.BlockSpec(memory_space=pltpu.VMEM)
    scores = pl.pallas_call(
        kernel,
        out_shape=jax.ShapeDtypeStruct((row_count // 128, 128), F32),
        in_specs=[vmem] * 3,
        out_specs=vmem,
        scratch_shapes=[
            pltpu.VMEM((row_count, width), BF16),
            pltpu.VMEM((8 * SLAB, 8, width), BF16),
            pltpu.VMEM((WINDOWS * CHUNK // 8, 8, width), BF16),
            pltpu.VMEM((WINDOWS, CHUNK, width), BF16),
            pltpu.VMEM((8, row_count), I32),
            pltpu.VMEM((8, row_count), I32),
            pltpu.VMEM((128, 128), BF16),
            pltpu.VMEM((8, 128), F32),
            pltpu.VMEM((3, 8, 128), F32),
            pltpu.VMEM((CHUNK, CHUNK), BF16),
            pltpu.VMEM((WINDOWS, CHUNK, 128), I32),
            pltpu.VMEM((WINDOWS, 8, CHUNK), I32),
            pltpu.VMEM((WINDOWS, CHUNK, 128), F32),
            pltpu.VMEM((WINDOWS, 8, CHUNK), F32),
            pltpu.VMEM((4, 8, CHUNK), F32),
            pltpu.VMEM((4, CHUNK, 128), F32),
            pltpu.VMEM((64, 128), F32),
            pltpu.VMEM((64, 128), F32),
            pltpu.SemaphoreType.DMA,
            pltpu.SemaphoreType.DMA((WINDOWS,)),
            pltpu.SemaphoreType.DMA((WINDOWS,)),
            pltpu.SemaphoreType.DMA((WINDOWS,)),
            pltpu.SemaphoreType.DMA((3,)),
            pltpu.SemaphoreType.DMA((3,)),
            pltpu.SemaphoreType.DMA,
            pltpu.SemaphoreType.DMA,
        ],
        compiler_params=pltpu.CompilerParams(collective_id=0, has_side_effects=True, vmem_limit_bytes=56 * 1024 * 1024),
    )(embeddings, route.reshape(row_count // 128, 128), cluster)
    return scores.reshape(row_count)


def solution(mesh):
    in_specs = (P(("grp", "blk"), None), P(("grp", "blk")), P("grp", "blk"))
    return jax.shard_map(on_device, mesh=mesh, in_specs=in_specs, out_specs=P(("grp", "blk")), check_vma=False)
```

```python
import functools

import jax
import jax.numpy as jnp
from jax import lax
from jax.experimental import pallas as pl
from jax.experimental.pallas import tpu as pltpu
from jax.sharding import PartitionSpec as P

MESH = pl.DeviceIdType.MESH
F32, BF16, I32 = jnp.float32, jnp.bfloat16, jnp.int32
SLAB = 40
USED = 36
WINDOWS = 8
CHUNK = 16 * SLAB


def dot(a, b):
    return lax.dot_general(a, b, (((1,), (0,)), ((), ())), preferred_element_type=F32)


def dot_t(a, b):
    return lax.dot_general(a, b, (((1,), (1,)), ((), ())), preferred_element_type=F32)


def iota(shape, dim):
    return lax.broadcasted_iota(I32, shape, dim)


def quotient(value, by):
    return jnp.floor((value + 0.5) * (1.0 / by))


def thirds(value):
    first = value.astype(BF16)
    rest = value - first.astype(F32)
    second = rest.astype(BF16)
    return first, second, (rest - second.astype(F32)).astype(BF16)


def window_shift(w):
    return (7 - w) // 2, (7 - w) % 2


def chip_of(u, v, e, x):
    return x, (u + x) % 4, (v + 2 * e + x) % 4


def device_of(x, y, z, core):
    return (y % 2) * 16 + z * 4 + x, (y // 2) * 2 + core


def kernel(
    emb_ref, route_ref, cluster_ref, out_ref,
    unit, send, rows, table, picks, ranks, meta, count, counts, spread, key_col, key_row, cl_col, cl_row, best, best_t, gone, back,
    send_sem, recv_sem, pass_sem, pass_send_sem, count_sem, count_send_sem, back_sem, back_send_sem,
):
    row_count, width = emb_ref.shape
    grp, blk = lax.axis_index("grp"), lax.axis_index("blk")
    me = grp * 4 + blk
    y_lo, z0, x0 = grp // 16, (grp // 4) % 4, grp % 4
    y0, core = (blk // 2) * 2 + y_lo, blk % 2
    u0, v0, e0 = (y0 - x0 + 4) % 4, (z0 - x0 + 4) % 2, ((z0 - x0 + 4) % 4) // 2
    sibling = (grp, blk + 1 - 2 * core)

    barrier = pltpu.get_barrier_semaphore()

    def greet(i, carry):
        other = ((me >> 1) + 1 + i) & 63
        pl.semaphore_signal(barrier, inc=1, device_id=(other >> 1, (other & 1) * 2 + v0), device_id_type=MESH)
        return carry

    def greet_more(i, carry):
        x = i & 3
        to = device_of(x, (i >> 2) & 3, (i >> 4) * 2 + ((core + x) & 1), 1 - v0)
        pl.semaphore_signal(barrier, inc=1, device_id=to, device_id_type=MESH)
        return carry

    lax.fori_loop(0, 63, greet, 0, unroll=9)
    lax.fori_loop(0, 32, greet_more, 0, unroll=8)

    @pl.when(v0 != core)
    def _():
        greet(63, 0)
        pl.semaphore_signal(barrier, inc=1, device_id=(grp, (blk + 2) % 4), device_id_type=MESH)

    values = emb_ref[...].astype(F32)
    unit[...] = (values * lax.rsqrt(jnp.sum(values * values, axis=1, keepdims=True) + 1e-06)).astype(BF16)

    route = jnp.concatenate([route_ref[k:k + 1, :] for k in range(row_count // 128)], axis=1).astype(F32)
    family = quotient(route, 6144)
    slot = route - family * 6144
    block = quotient(slot, 1536)
    slot_hi = quotient(slot, 48)
    slot_lo = slot - slot_hi * 48
    family_int = family.astype(I32)
    fam_y, fam_z, fam_x = family_int >> 4, (family_int >> 2) & 3, family_int & 3

    def order_number(y):
        dx, dy, dz = (fam_x - x0) & 3, (y - y0) & 3, (fam_z - z0) & 3
        du, dzx = (dy - dx) & 3, (dz - dx) & 3
        return (7 - du * 2 - (dzx & 1)) * 8 + (1 - (dzx >> 1)) * 4 + 3 - dx

    pick_a = jnp.where(block < 2.5, order_number(fam_y), -1)
    pick_b = jnp.where(block > 0.5, order_number(fam_y + 2), -1)
    slab_iota = iota((64, row_count), 0)
    hot_a = (slab_iota == pick_a).astype(F32)
    hot_b = (slab_iota == pick_b).astype(F32)
    hot = (hot_a + hot_b).astype(BF16)
    earlier = (iota((256, 256), 0) < iota((256, 256), 1)).astype(F32).astype(BF16)
    before = jnp.zeros((64, 1), F32)
    prefix = []
    for k in range(row_count // 256):
        part = hot[:, k * 256:(k + 1) * 256]
        prefix.append(dot(part, earlier) + before)
        before = before + jnp.sum(part.astype(F32), axis=1, keepdims=True)
    prefix = jnp.concatenate(prefix, axis=1)
    rank_a = jnp.sum(hot_a * prefix, axis=0, keepdims=True).astype(I32)
    rank_b = jnp.sum(hot_b * prefix, axis=0, keepdims=True).astype(I32)
    picks[0:1, :], picks[1:2, :] = pick_a, pick_b
    ranks[0:1, :], ranks[1:2, :] = rank_a, rank_b
    lane_iota = iota((128, row_count), 0)
    hi = jnp.zeros((64, 128), F32)
    lo = jnp.zeros((64, 128), F32)
    for hot_one, rank in ((hot_a, rank_a), (hot_b, rank_b)):
        chosen = lane_iota == rank
        hi = hi + dot_t(hot_one.astype(BF16), jnp.where(chosen, slot_hi, 0.0).astype(BF16))
        lo = lo + dot_t(hot_one.astype(BF16), jnp.where(chosen, slot_lo, 0.0).astype(BF16))
    meta[0:64, :] = hi.astype(BF16)
    meta[64:128, :] = lo.astype(BF16)

    cluster = cluster_ref[...]
    which = iota((8, 128), 0)
    tally = jnp.zeros((8, 128), F32)
    for k in range(1, 4):
        below = jnp.sum((cluster < k).astype(F32), axis=1, keepdims=True)
        tally = jnp.where(which == k, below, tally)
    count[...] = tally

    @pl.when(v0 == core)
    def _():
        pl.semaphore_wait(barrier, 95)

    @pl.when(v0 != core)
    def _():
        pl.semaphore_wait(barrier, 97)

    def count_copy(step):
        return pltpu.make_async_remote_copy(
            src_ref=count, dst_ref=counts.at[step], send_sem=count_send_sem.at[step], recv_sem=count_sem.at[step],
            device_id=(grp, (blk + 1 + step) % 4), device_id_type=MESH,
        )

    for step in range(3):
        count_copy(step).start()

    target_a = jnp.where(pick_a >= 0, pick_a * SLAB + rank_a, -1)
    target_b = jnp.where(pick_b >= 0, pick_b * SLAB + rank_b, -1)
    picks[2:3, :], picks[3:4, :] = target_a, target_b
    home_row = ((v0 * 4 + u0) * 16 + (e0 * 4 + x0) * 2 + core) * (SLAB // 8)
    p_col = iota((8 * SLAB, 128), 0).astype(F32)
    p_slab = quotient(p_col, SLAB)
    p_in = (p_col - p_slab * SLAB).astype(I32)
    p_slab = p_slab.astype(I32)
    p_lane = iota((8 * SLAB, 128), 1)

    def make_window(w, carry):
        p_iota = iota((8 * SLAB, row_count), 0) + w * (8 * SLAB)
        one_hot = ((p_iota == picks[2:3, :]) | (p_iota == picks[3:4, :])).astype(F32).astype(BF16)
        body = dot(one_hot, unit[...])
        slab_no = p_slab + w * 8
        info_hot = (((p_in == USED) & (p_lane == slab_no)) | ((p_in == USED + 1) & (p_lane == slab_no + 64))).astype(F32).astype(BF16)
        info = dot(info_hot, meta[...])
        base = w * SLAB
        body = jnp.concatenate([body[:, 0:128] + info, body[:, 128:width]], axis=1).astype(BF16)
        send[pl.ds(base, SLAB)] = body.reshape(SLAB, 8, width)
        du, dv = window_shift(w)

        def send_one(k, inner):
            dx, dy, dz = chip_of(du, dv, 1 - k // 4, 3 - k % 4)
            to = device_of((x0 + dx) % 4, (y0 + dy) % 4, (z0 + dz) % 4, v0)
            source = send.at[pl.ds((w * 8 + k) * (SLAB // 8), SLAB // 8)]
            here = (to[0] * 4 + to[1]) == me

            @pl.when(jnp.logical_not(here))
            def _():
                pltpu.make_async_remote_copy(
                    src_ref=source, dst_ref=rows.at[pl.ds(home_row, SLAB // 8)], send_sem=send_sem, recv_sem=recv_sem.at[w],
                    device_id=to, device_id_type=MESH,
                ).start()

            @pl.when(here)
            def _():
                pltpu.make_async_copy(source, rows.at[pl.ds(home_row, SLAB // 8)], recv_sem.at[w]).start()

            return inner

        lax.fori_loop(0, 8, send_one, 0, unroll=4)
        return carry

    lax.fori_loop(0, WINDOWS, make_window, 0)

    p = iota((CHUNK, 128), 0).astype(F32)
    slab_of = quotient(p, SLAB)
    in_slab = p - slab_of * SLAB
    diagonal = ((iota((CHUNK, 128), 1).astype(F32) == in_slab) & (in_slab < USED)).astype(F32)
    other = iota((CHUNK, CHUNK), 1).astype(F32)
    p_wide = iota((CHUNK, CHUNK), 0).astype(F32)
    first = quotient(p_wide, SLAB) * SLAB
    spread[...] = jnp.where(other == first + USED, 48.0, jnp.where(other == first + (USED + 1), 1.0, 0.0)).astype(BF16)

    def data_key(slab_no, inside, u, v):
        sx, se, sc = (slab_no >> 1) & 3, slab_no >> 3, slab_no & 1
        sy, sz = (u + sx) & 3, (v + 2 * se + sx) & 3
        source = ((sy & 1) * 16 + sz * 4 + sx) * 4 + (sy >> 1) * 2 + sc
        return source * SLAB + inside

    slab_col, in_col = slab_of.astype(I32), in_slab.astype(I32)
    q = iota((8, CHUNK), 1).astype(F32)
    slab_row = quotient(q, SLAB)
    in_row = (q - slab_row * SLAB).astype(I32)
    slab_row = slab_row.astype(I32)

    def make_keys(k, carry):
        key_col[k] = data_key(slab_col, in_col, k % 4, k // 4)
        key_row[k] = data_key(slab_row, in_row, k % 4, k // 4)
        return carry

    lax.fori_loop(0, WINDOWS, make_keys, 0)
    best[...] = jnp.full(best.shape, -1.0, F32)
    best_t[...] = jnp.full(best_t.shape, -1.0, F32)

    total = count[...]
    for step in range(3):
        count_copy(step).wait()
        total = total + counts[step]
    ends = [total[k:k + 1, :] for k in range(1, 4)]
    ones_col = jnp.ones((128, 128), BF16)
    ones_row = jnp.ones((8, 128), BF16)

    def chunk_of(w):
        du, dv = window_shift(w)
        u, v = (u0 - du + 4) % 4, (v0 - dv + 2) % 2
        return v * 4 + u, v

    def pass_copy(w, chunk):
        part = rows.at[pl.ds(chunk * (CHUNK // 8), CHUNK // 8)]
        return pltpu.make_async_remote_copy(
            src_ref=part, dst_ref=part, send_sem=pass_send_sem.at[w], recv_sem=pass_sem.at[w],
            device_id=sibling, device_id_type=MESH,
        )

    def fold(mine, others, both=False):
        x_mine = table[mine]
        x_other = table[others]
        scores = dot_t(x_other, x_mine)
        wide = lambda a: jnp.concatenate([a] * (CHUNK // 128), axis=1)
        same = wide(cl_col[others]) == cl_row[mine][0:1, :]
        prior = wide(key_col[others]) < key_row[mine][0:1, :]
        held = jnp.where(same & prior, scores, -1.0).reshape(CHUNK // 8, 8, CHUNK)
        u = mine % 4
        best[u] = jnp.maximum(best[u], jnp.max(held, axis=0))
        if both:
            later = jnp.where(same & jnp.logical_not(prior), scores, -1.0)
            most = later[:, 0:128]
            for k in range(1, CHUNK // 128):
                most = jnp.maximum(most, later[:, k * 128:(k + 1) * 128])
            t = others % 4
            best_t[t] = jnp.maximum(best_t[t], most)

    def take_window(w, carry):
        chunk, v = chunk_of(w)
        part = rows.at[pl.ds(chunk * (CHUNK // 8), CHUNK // 8)]

        @pl.when(v == core)
        def _():
            pltpu.make_async_copy(part, part, recv_sem.at[w]).wait()
            pass_copy(w, chunk).start()

        @pl.when(v != core)
        def _():
            pltpu.make_async_copy(part, part, pass_sem.at[w]).wait()

        table[chunk] = rows[pl.ds(chunk * (CHUNK // 8), CHUNK // 8)].reshape(CHUNK, width)
        slots = dot(spread[...], table[chunk][:, 0:128])
        number = 1.0
        for end in ends:
            number = number + (slots >= end).astype(F32)
        number = (number * diagonal).astype(BF16)
        cl_col[chunk] = dot(number, ones_col)
        cl_row[chunk] = dot_t(ones_row, number)

        def with_earlier(k, inner):
            chunk_k, v_k = chunk_of(k)

            @pl.when((v == core) & ((v_k != core) | (k == w)))
            def _():
                fold(chunk, chunk_k)

            @pl.when((v == core) & (v_k == core) & (k < w))
            def _():
                fold(chunk, chunk_k, both=True)

            @pl.when((v != core) & (v_k == core))
            def _():
                fold(chunk_k, chunk)

            return inner

        lax.fori_loop(0, w + 1, with_earlier, 0)
        return carry

    lax.fori_loop(0, WINDOWS, take_window, 0)

    slab_lane = quotient(iota((16, CHUNK), 1).astype(F32), SLAB)
    own_slab = slab_lane == iota((16, CHUNK), 0).astype(F32)
    as_slabs = own_slab.astype(F32).astype(BF16)
    fold_lanes = (diagonal > 0.5).astype(F32).astype(BF16)

    def give_back(u, carry):
        row = jnp.max(best[u], axis=0, keepdims=True)
        picked = jnp.where(own_slab, row, 0.0)
        table = sum(dot(piece, fold_lanes) for piece in thirds(picked))
        listed = jnp.where(diagonal > 0.5, jnp.max(best_t[u], axis=1, keepdims=True), 0.0)
        table_t = sum(dot(as_slabs, piece) for piece in thirds(listed))
        gone[pl.ds(pl.multiple_of(u * 16, 16), 16), :] = jnp.maximum(table, table_t)

        def one(k, inner):
            sx, sy, sz = chip_of(u, core, k // 8, (k // 2) % 4)
            to = device_of(sx, sy, sz, k % 2)
            dx, dy, dz = (x0 - sx + 4) % 4, (y0 - sy + 4) % 4, (z0 - sz + 4) % 4
            du, dzx = (dy - dx + 4) % 4, (dz - dx + 4) % 4
            number = (7 - du * 2 - dzx % 2) * 8 + (1 - dzx // 2) * 4 + 3 - dx
            here = (to[0] * 4 + to[1]) == me

            @pl.when(jnp.logical_not(here))
            def _():
                pltpu.make_async_remote_copy(
                    src_ref=gone.at[pl.ds(u * 16 + k, 1)], dst_ref=back.at[pl.ds(number, 1)], send_sem=back_send_sem, recv_sem=back_sem,
                    device_id=to, device_id_type=MESH,
                ).start()

            @pl.when(here)
            def _():
                pltpu.make_async_copy(gone.at[pl.ds(u * 16 + k, 1)], back.at[pl.ds(number, 1)], back_sem).start()

            return inner

        lax.fori_loop(0, 16, one, 0, unroll=4)
        return carry

    lax.fori_loop(0, 4, give_back, 0)

    mine_too = v0 == core

    @pl.when(mine_too)
    def _():
        pltpu.make_async_copy(send.at[pl.ds(0, 63 * (SLAB // 8))], send.at[pl.ds(0, 63 * (SLAB // 8))], send_sem).wait()

    @pl.when(jnp.logical_not(mine_too))
    def _():
        pltpu.make_async_copy(send, send, send_sem).wait()

    def pass_sent(w, carry):
        chunk, v = chunk_of(w)

        @pl.when(v == core)
        def _():
            pass_copy(w, chunk).wait_send()

        return carry

    lax.fori_loop(0, WINDOWS, pass_sent, 0)

    pltpu.make_async_copy(back, back, back_sem).wait()
    result = jnp.full((1, row_count), -1.0, F32)
    got = jnp.concatenate([back[...], jnp.zeros((64, 128), F32)], axis=0).T
    pieces = thirds(got[:, 0:64])
    for k in range(2):
        hot_one = (slab_iota == picks[k:k + 1, :]).astype(F32).astype(BF16)
        table = sum(dot(piece, hot_one) for piece in pieces)
        mark = (lane_iota == ranks[k:k + 1, :]) & (picks[k:k + 1, :] >= 0)
        result = jnp.maximum(result, jnp.max(jnp.where(mark, table, -1.0), axis=0, keepdims=True))
    for k in range(row_count // 128):
        out_ref[k:k + 1, :] = result[:, k * 128:(k + 1) * 128]

    @pl.when(v0 == core)
    def _():
        pltpu.make_async_copy(gone.at[pl.ds(0, 63)], gone.at[pl.ds(0, 63)], back_send_sem).wait()

    @pl.when(v0 != core)
    def _():
        pltpu.make_async_copy(gone, gone, back_send_sem).wait()


def on_device(embeddings, route, cluster):
    row_count, width = embeddings.shape
    vmem = pl.BlockSpec(memory_space=pltpu.VMEM)
    scores = pl.pallas_call(
        kernel,
        out_shape=jax.ShapeDtypeStruct((row_count // 128, 128), F32),
        in_specs=[vmem] * 3,
        out_specs=vmem,
        scratch_shapes=[
            pltpu.VMEM((row_count, width), BF16),
            pltpu.VMEM((8 * SLAB, 8, width), BF16),
            pltpu.VMEM((WINDOWS * CHUNK // 8, 8, width), BF16),
            pltpu.VMEM((WINDOWS, CHUNK, width), BF16),
            pltpu.VMEM((8, row_count), I32),
            pltpu.VMEM((8, row_count), I32),
            pltpu.VMEM((128, 128), BF16),
            pltpu.VMEM((8, 128), F32),
            pltpu.VMEM((3, 8, 128), F32),
            pltpu.VMEM((CHUNK, CHUNK), BF16),
            pltpu.VMEM((WINDOWS, CHUNK, 128), I32),
            pltpu.VMEM((WINDOWS, 8, CHUNK), I32),
            pltpu.VMEM((WINDOWS, CHUNK, 128), F32),
            pltpu.VMEM((WINDOWS, 8, CHUNK), F32),
            pltpu.VMEM((4, 8, CHUNK), F32),
            pltpu.VMEM((4, CHUNK, 128), F32),
            pltpu.VMEM((64, 128), F32),
            pltpu.VMEM((64, 128), F32),
            pltpu.SemaphoreType.DMA,
            pltpu.SemaphoreType.DMA((WINDOWS,)),
            pltpu.SemaphoreType.DMA((WINDOWS,)),
            pltpu.SemaphoreType.DMA((WINDOWS,)),
            pltpu.SemaphoreType.DMA((3,)),
            pltpu.SemaphoreType.DMA((3,)),
            pltpu.SemaphoreType.DMA,
            pltpu.SemaphoreType.DMA,
        ],
        compiler_params=pltpu.CompilerParams(collective_id=0, has_side_effects=True, vmem_limit_bytes=56 * 1024 * 1024),
    )(embeddings, route.reshape(row_count // 128, 128), cluster)
    return scores.reshape(row_count)


def solution(mesh):
    in_specs = (P(("grp", "blk"), None), P(("grp", "blk")), P("grp", "blk"))
    return jax.shard_map(on_device, mesh=mesh, in_specs=in_specs, out_specs=P(("grp", "blk")), check_vma=False)
```
